256 devices in a mesh: tile: 16 (over z, core), tm: 16 (over x, y).
Axes of the slice: x: 4, y: 4, z: 8, core: 2. Of those that a mesh axis runs over, the one named last changes fastest.
Arguments:
- src_snap: bfloat16 [256, 32, 128, 256], P('tile', 'tm'), may hold values from -6 to 6
- rcv_snap: bfloat16 [256, 32, 128, 256], P('tile', 'tm'), may hold values from -6 to 6
- q_rate: float32 [256], replicated, may hold values from 0.05 to 1.5
- nbr_device: int32 [256, 2], replicated, may hold values from 0 to 15, all different within a row; in each aligned block of 16 rows (0 to 15, 16 to 31, ...) at most 3 rows name the same one
- nbr_index: int32 [256, 2], replicated, may hold values from 0 to 15
- depth_extent: int32 [256], P('tile'), may hold values from 16 to 256, as said below
Outputs:
- image: float32 [256, 8, 49, 256], P(('tile', 'tm'))
The draws below stay inside these ranges and needn't reach their ends.
Inputs may be any that keep to these rules, and one draw needn't show every extreme that they name: `nbr_device`: the two devices of a row differ; among the rows of one device (aligned blocks of 16 rows) no device is named more than 3 times, and in some device's rows one device is named exactly 3 times. Cells of a tile's gathers at depth depth_extent[s] and below are zero.
All inputs are finite; a program needn't handle non-finite values.
Results may differ from the reference program's by a relative error of at most 0.0003.
Values may be sent and summed in bfloat16 or wider, within the bound.
No kernel may reach another device: no remote copies, remote signals or barrier semaphores. Data moves between devices by JAX's collectives and lax.ppermute only.
A program may use at most 128 MiB of HBM per device.

```python
import math
import jax
import jax.numpy as jnp
import numpy as np
from jax import lax

TPD = 16
Z = 256
BW = 128
GSTEP = 16
HMAX = 24
SLOTS = 256
TIMES = 32
GB = 8
OFFS = 49
RIM_L = 16
RIM_R = 17
CAP = 3
N_TILE = 16


def draw_depth_extent(key, part):
    key_deep, key_low, key_high, key_pick, key_other = jax.random.split(key, 5)
    device_count = SLOTS // TPD
    shallow_limit = max(1, Z // 16)
    deep_flag = jax.random.randint(key_deep, (device_count,), 0, 2)
    shallow = jax.random.randint(key_low, (SLOTS,), shallow_limit, Z // 2 + 1)
    deeper = jax.random.randint(key_high, (SLOTS,), Z // 2 + 1, Z + 1)
    owner_device = jnp.arange(SLOTS) // TPD
    extent = jnp.where(deep_flag[owner_device] == 1, deeper, shallow)
    chosen = jax.random.randint(key_pick, (), 0, SLOTS)
    other_pick = (chosen + 1 + jax.random.randint(key_other, (), 0, SLOTS - 1)) % SLOTS
    extent = extent.at[chosen].set(Z).at[other_pick].set(shallow_limit)
    return extent.astype(jnp.int32)


def plant(values, own_key, low, top_value):
    place = [jax.random.randint(jax.random.fold_in(own_key, axis), (), 0, length) for axis, length in enumerate(values.shape)]
    longest = values.shape.index(max(values.shape))
    next_to = place[:longest] + [(place[longest] + 1) % values.shape[longest]] + place[longest + 1:]
    return values.at[tuple(place)].set(low).at[tuple(next_to)].set(top_value)


def block_scale(own_key, shape, cuts, least, largest):
    loudness, own = 1.0, jax.random.fold_in(own_key, 6)
    for axis_at, shards_of in cuts:
        heights = jnp.exp(jax.random.uniform(jax.random.fold_in(own, axis_at), (shards_of,), jnp.float32, least / len(cuts), largest / len(cuts)))
        loudness = loudness * jnp.repeat(heights, shape[axis_at] // shards_of).reshape([-1 if axis == axis_at else 1 for axis in range(len(shape))])
    return loudness


def shared_out(key, own, number, rows, amount, top, reach, slope):
    sequence = jax.random.permutation(key, amount)
    heavy_load, usual = shares(amount, rows * top, reach, slope, True), shares(amount, rows * top, reach, slope, False)
    places = jnp.arange(amount)

    def named(sizes, rotation):
        used = int((sizes > 0).sum())
        fixed = max(1, used // 4)
        shifted = fixed + (places - fixed + rotation * (used - fixed)) % max(1, amount - fixed)
        return jnp.zeros((amount,), jnp.int32).at[sequence[jnp.where(places < fixed, places, shifted)]].set(jnp.asarray(sizes, jnp.int32))

    sizes = jnp.where(number % 4 == 0, named(heavy_load, number // 4), named(usual, number - number // 4 - 1))
    mixed = jax.random.permutation(jax.random.fold_in(own, 3), amount)
    source_of, receiver = mixed[0:amount // 2 * 2:2], mixed[1:amount // 2 * 2:2]
    margin = jnp.minimum(sizes[source_of] - 1, reach - sizes[receiver]) // 2
    margin = jnp.where((source_of == sequence[0]) | (receiver == sequence[0]) | (sizes[receiver] == 0), 0, jnp.maximum(margin, 0))
    shifted = jax.random.randint(jax.random.fold_in(own, 4), (amount // 2,), 0, 1 << 20) % (margin + 1)
    sizes = sizes.at[source_of].add(-shifted).at[receiver].add(shifted)
    labels = jnp.searchsorted(jnp.cumsum(sizes), jnp.arange(rows * top), side="right").astype(jnp.int32)
    listing = labels.reshape(top, rows).T
    listing = listing[jax.random.permutation(jax.random.fold_in(own, 1), rows)]
    rotation = jax.random.randint(jax.random.fold_in(own, 2), (rows, 1), 0, top)
    return jnp.take_along_axis(listing, (jnp.arange(top)[None, :] + rotation) % top, axis=1)


def shares(number_of, total, most, slope, full):
    weights = [(1 << 20) // math.isqrt(rank ** slope) + 1 for rank in range(1, number_of + 1)]
    largest = most if full else min(most, max(-(-total // number_of), total * weights[0] // sum(weights)))
    least = 1 if total - largest >= number_of - 1 else 0
    given, rest = [largest] + [least] * (number_of - 1), total - largest - least * (number_of - 1)
    while rest > 0:
        free = [i for i in range(1, number_of) if given[i] < largest] or [i for i in range(1, number_of) if given[i] < most]
        pool, left = sum([weights[i] for i in free]), rest
        for i in free:
            extra = min(most - given[i], max(1, left * weights[i] // pool), rest)
            given[i] = given[i] + extra
            rest = rest - extra
    return np.array(given)


def normal_values(key, dims, deviation, reach, pieces=(), kind=jnp.bfloat16):
    level = block_scale(key, dims, pieces, -0.22, 0.18) if pieces else 1.0
    result = jax.random.normal(key, dims, jnp.float32) * deviation * level
    return jnp.minimum(jnp.maximum(result, -reach), reach).astype(kind)


def setup_inputs(seed: int = 0) -> dict:
    splits = jax.random.split(jax.random.key(seed), 7)
    src_snap = normal_values(splits[0], (SLOTS, TIMES, BW, Z), 1.0, 6.0, ((0, 16), (1, 16)))
    rcv_snap = normal_values(splits[1], (SLOTS, TIMES, BW, Z), 1.0, 6.0, ((0, 16), (1, 16)))
    q_rate = jnp.clip(jnp.exp(jax.random.uniform(splits[2], (Z,), jnp.float32, math.log(0.05), math.log(1.5))), 0.05, 1.5)
    nbr_device_keys = jax.random.split(jax.random.fold_in(splits[3], 1), SLOTS // TPD)
    nbr_device_turns = jax.random.permutation(jax.random.fold_in(splits[3], 3), SLOTS // TPD)
    nbr_device = jax.vmap(lambda own, number: shared_out(jax.random.fold_in(splits[3], 2), own, number, TPD, N_TILE, 2, CAP, 0))(nbr_device_keys, nbr_device_turns).reshape((SLOTS, 2))
    nbr_index = plant(jax.random.randint(splits[4], (SLOTS, 2), 0, TPD), jax.random.fold_in(splits[4], 1), 0, TPD - 1).astype(jnp.int32)
    depth_extent = draw_depth_extent(jax.random.fold_in(splits[6], 71), 0)
    return {"src_snap": src_snap, "rcv_snap": rcv_snap, "q_rate": q_rate, "nbr_device": nbr_device, "nbr_index": nbr_index, "depth_extent": depth_extent}


def reference(src_snap, rcv_snap, q_rate, nbr_device, nbr_index, depth_extent):
    time_steps = jnp.arange(TIMES).astype(jnp.float32)
    weight = jnp.exp(q_rate[None, :] * time_steps[:, None] / TIMES)
    norm_scale = 1.0 / math.sqrt(TIMES)
    depth_index = jnp.arange(Z).astype(jnp.int32)
    begins = [RIM_L + GSTEP * gather + GSTEP // 2 - HMAX for gather in range(GB)]

    def one_tile(slot):
        left_slot = nbr_device[slot, 0] * TPD + nbr_index[slot, 0]
        right_slot = nbr_device[slot, 1] * TPD + nbr_index[slot, 1]

        def strip(field):
            return jnp.concatenate([field[left_slot][:, BW - RIM_L:, :], field[slot], field[right_slot][:, :RIM_R, :]], axis=1)
        src_strip = strip(src_snap).astype(jnp.float32)
        rcv_strip = strip(rcv_snap).astype(jnp.float32)
        src_window = jnp.stack([src_strip[:, begin:begin + OFFS, :] for begin in begins], axis=1)[:, :, ::-1, :]
        rcv_window = jnp.stack([rcv_strip[:, begin:begin + OFFS, :] for begin in begins], axis=1)
        total = lax.optimization_barrier(jnp.sum(src_window * rcv_window * weight[:, None, None, :], axis=0))
        depth_mask = (depth_index < depth_extent[slot]).astype(jnp.float32)
        return total * norm_scale * depth_mask[None, None, :]
    return lax.map(one_tile, jnp.arange(SLOTS).astype(jnp.int32))
```

```python
import functools
import math

import jax
import jax.numpy as jnp
from jax import lax
from jax.experimental import pallas as pl
from jax.experimental.pallas import tpu as pltpu
from jax.sharding import PartitionSpec as P

GSTEP = 16
GB = 8
OFFS = 49
RIM = 16
BODY = OFFS - 1


def pack_kernel(send_ref, src_lo, src_hi, rcv_lo, rcv_hi, out_ref, *, slots, steps):
    dest = pl.program_id(0)
    depth = out_ref.shape[2]
    tail = out_ref.shape[1] - slots * 2 * steps * RIM
    row_ids = lax.broadcasted_iota(jnp.int32, (tail, depth), 0)
    extra = jnp.zeros((tail, depth), jnp.float32)
    for slot in range(slots):
        choice = send_ref[dest * slots + slot]
        index = choice // 2
        right = choice % 2
        for field, (low, high) in enumerate(((src_lo, src_hi), (rcv_lo, rcv_hi))):
            for step in range(steps):
                at = (slot * 2 + field) * steps + step
                rows = low[index, step]
                rim = jnp.where(right == 1, rows[:RIM], high[index, step])
                out_ref[0, at * RIM : (at + 1) * RIM, :] = rim
                beyond = rows[RIM : RIM + 8].astype(jnp.float32)[0:1]
                extra = jnp.where(row_ids == at, beyond, extra)
    out_ref[0, slots * 2 * steps * RIM :, :] = extra.astype(out_ref.dtype)


def pack(send, src_snap, rcv_snap, slots):
    tiles, steps, width, depth = src_snap.shape
    devices = send.shape[0] // slots
    parts = slots * 2 * steps
    rows = parts * RIM + -(-parts // 16) * 16
    low = pl.BlockSpec((tiles, steps, RIM + 8, depth), lambda i, s: (0, 0, 0, 0))
    high = pl.BlockSpec((tiles, steps, RIM, depth), lambda i, s: (0, 0, width // RIM - 1, 0))
    return pl.pallas_call(
        functools.partial(pack_kernel, slots=slots, steps=steps),
        name="pack_rims",
        grid_spec=pltpu.PrefetchScalarGridSpec(
            num_scalar_prefetch=1,
            grid=(devices,),
            in_specs=[low, high, low, high],
            out_specs=pl.BlockSpec((1, rows, depth), lambda i, s: (i, 0, 0)),
        ),
        out_shape=jax.ShapeDtypeStruct((devices, rows, depth), src_snap.dtype),
    )(send, src_snap, src_snap, rcv_snap, rcv_snap)


def unpack_kernel(arrival_ref, in_ref, out_ref, *, slots, steps):
    tile = pl.program_id(0)
    rows = 2 * steps * RIM
    left = arrival_ref[2 * tile]
    right = arrival_ref[2 * tile + 1]
    left_device, left_slot = left // slots, left % slots
    right_device, right_slot = right // slots, right % slots
    out_ref[0, 0:rows, :] = in_ref[left_device, pl.ds(pl.multiple_of(left_slot * rows, 16), rows), :]
    out_ref[0, rows : 2 * rows, :] = in_ref[
        right_device, pl.ds(pl.multiple_of(right_slot * rows, 16), rows), :
    ]
    tail = in_ref[right_device, slots * rows :, :].astype(jnp.float32)
    count = 2 * steps
    picked = tail[0:count]
    for slot in range(1, slots):
        picked = jnp.where(right_slot == slot, tail[slot * count : (slot + 1) * count], picked)
    padded = jnp.concatenate([picked, jnp.zeros((8 - count, picked.shape[1]), jnp.float32)], axis=0)
    out_ref[0, 2 * rows :, :] = padded.astype(out_ref.dtype)


def unpack(arrival, received, slots, tiles, steps):
    devices, in_rows, depth = received.shape
    rows = 2 * (2 * steps * RIM) + 8
    return pl.pallas_call(
        functools.partial(unpack_kernel, slots=slots, steps=steps),
        name="unpack_rims",
        grid_spec=pltpu.PrefetchScalarGridSpec(
            num_scalar_prefetch=1,
            grid=(tiles,),
            in_specs=[pl.BlockSpec((devices, in_rows, depth), lambda i, s: (0, 0, 0))],
            out_specs=pl.BlockSpec((1, rows, depth), lambda i, s: (i, 0, 0)),
        ),
        out_shape=jax.ShapeDtypeStruct((tiles, rows, depth), received.dtype),
    )(arrival, received)


def image_kernel(
    extent_ref, q_ref, src_ref, rcv_ref, rim_ref, out_ref, rev_ref, fwd_ref, body_ref, last_ref, *, total_steps
):
    block = pl.program_id(0)
    parts, steps, width, depth = src_ref.shape
    strip = width + 2 * RIM
    rows = 2 * steps * RIM

    @pl.when(block == 0)
    def _():
        body_ref[...] = jnp.zeros_like(body_ref)
        last_ref[...] = jnp.zeros_like(last_ref)

    out_rows = rev_ref.shape[1]
    out_id = lax.broadcasted_iota(jnp.int32, (out_rows, strip), 0)
    in_id = lax.broadcasted_iota(jnp.int32, (out_rows, strip), 1)
    flip = (out_id <= strip) & (in_id == strip - out_id)
    pick = (out_id >= strip + 8) & (in_id == (out_id - (strip + 8)) * GSTEP)
    select = (flip | pick).astype(src_ref.dtype)

    end_out = lax.broadcasted_iota(jnp.int32, (GB, strip), 0)
    end_in = lax.broadcasted_iota(jnp.int32, (GB, strip), 1)
    end_pick = (end_in == end_out * GSTEP + BODY).astype(src_ref.dtype)
    end_id = lax.broadcasted_iota(jnp.int32, (GB, depth), 0)

    for part in range(parts):
        beyond = rim_ref[part, 2 * rows :, :].astype(jnp.float32)
        for step in range(steps):
            at = part * steps + step
            src_at, rcv_at = step * RIM, (steps + step) * RIM
            src_strip = jnp.concatenate(
                [
                    rim_ref[part, src_at : src_at + RIM, :],
                    src_ref[part, step],
                    rim_ref[part, rows + src_at : rows + src_at + RIM, :],
                ],
                axis=0,
            )
            rev_ref[at] = jnp.dot(select, src_strip, preferred_element_type=jnp.float32)
            rev_ref[at, 0:1, :] = beyond[step : step + 1]
            time = ((block * parts + part) * steps + step).astype(jnp.float32)
            weight = jnp.exp(q_ref[...] * time / total_steps)
            rcv_strip = jnp.concatenate(
                [
                    rim_ref[part, rcv_at : rcv_at + RIM, :],
                    rcv_ref[part, step],
                    rim_ref[part, rows + rcv_at : rows + rcv_at + RIM, :],
                ],
                axis=0,
            )
            fwd_ref[at, 0:strip, :] = rcv_strip.astype(jnp.float32) * weight
            ends = jnp.dot(end_pick, rcv_strip, preferred_element_type=jnp.float32)
            ends = jnp.where(end_id == GB - 1, beyond[steps + step : steps + step + 1], ends)
            fwd_ref[at, strip : strip + GB, :] = ends * weight

    many = parts * steps
    for gather in range(GB):
        rev_at = strip - BODY - GSTEP * gather
        fwd_at = GSTEP * gather
        total = body_ref[gather]
        for at in range(many):
            total += rev_ref[at, rev_at : rev_at + BODY, :] * fwd_ref[at, fwd_at : fwd_at + BODY, :]
        body_ref[gather] = total
    total = last_ref[...]
    for at in range(many):
        total += rev_ref[at, strip + 8 : strip + 16, :] * fwd_ref[at, strip : strip + GB, :]
    last_ref[...] = total

    @pl.when(block == pl.num_programs(0) - 1)
    def _():
        depth_id = lax.broadcasted_iota(jnp.int32, (1, depth), 1)
        scale = jnp.where(depth_id < extent_ref[0], 1.0, 0.0) * (1.0 / math.sqrt(total_steps))
        for gather in range(GB):
            out_ref[0, gather, 0:BODY, :] = body_ref[gather] * scale
            out_ref[0, gather, BODY:OFFS, :] = last_ref[gather : gather + 1, :] * scale


def image(extent, q_rate, src_all, rcv_all, rim_all):
    devices, steps, width, depth = src_all.shape
    parts = 2
    strip = width + 2 * RIM
    total_steps = devices * steps
    main = pl.BlockSpec((parts, steps, width, depth), lambda i, s: (i, 0, 0, 0))
    return pl.pallas_call(
        functools.partial(image_kernel, total_steps=total_steps),
        name="image_tile",
        grid_spec=pltpu.PrefetchScalarGridSpec(
            num_scalar_prefetch=1,
            grid=(devices // parts,),
            in_specs=[
                pl.BlockSpec((1, depth), lambda i, s: (0, 0)),
                main,
                main,
                pl.BlockSpec((parts, rim_all.shape[1], depth), lambda i, s: (i, 0, 0)),
            ],
            out_specs=pl.BlockSpec((1, GB, OFFS, depth), lambda i, s: (0, 0, 0, 0)),
            scratch_shapes=[
                pltpu.VMEM((parts * steps, strip + 16, depth), jnp.float32),
                pltpu.VMEM((parts * steps, strip + 8, depth), jnp.float32),
                pltpu.VMEM((GB, BODY, depth), jnp.float32),
                pltpu.VMEM((GB, depth), jnp.float32),
            ],
        ),
        out_shape=jax.ShapeDtypeStruct((1, GB, OFFS, depth), jnp.float32),
    )(extent, q_rate.reshape(1, depth), src_all, rcv_all, rim_all)


def routes(nbr_device, nbr_index, device_count, tile_count, slots, own_index):
    requests = 2 * tile_count
    device = nbr_device.reshape(device_count, requests)
    code = nbr_index.reshape(device_count, requests) * 2 + jnp.arange(requests, dtype=jnp.int32) % 2
    ids = jnp.arange(requests, dtype=jnp.int32)
    named = device == own_index
    rank = jnp.sum((named[:, None, :] & (ids[None, :] < ids[:, None])).astype(jnp.int32), axis=2)
    hit = named[:, None, :] & (rank[:, None, :] == jnp.arange(slots, dtype=jnp.int32)[None, :, None])
    send = jnp.sum(jnp.where(hit, code[:, None, :], 0), axis=2).reshape(-1)
    mine = lax.dynamic_slice_in_dim(device, own_index, 1, 0)[0]
    same = (mine[:, None] == mine[None, :]) & (ids[None, :] < ids[:, None])
    arrival = mine * slots + jnp.sum(same.astype(jnp.int32), axis=1)
    return send, arrival


def local(src_snap, rcv_snap, q_rate, nbr_device, nbr_index, depth_extent):
    tile_count, step_count, _, _ = src_snap.shape
    device_count = lax.axis_size("tile")
    slots = (2 * tile_count + device_count - 1) // device_count + 1
    send, arrival = routes(
        nbr_device, nbr_index, device_count, tile_count, slots, lax.axis_index("tile")
    )
    src_all = lax.all_to_all(src_snap, "tm", split_axis=0, concat_axis=0, tiled=True)
    rcv_all = lax.all_to_all(rcv_snap, "tm", split_axis=0, concat_axis=0, tiled=True)
    packed = pack(send, src_snap, rcv_snap, slots)
    received = lax.all_to_all(packed, "tile", split_axis=0, concat_axis=0, tiled=True)
    rims = unpack(arrival, received, slots, tile_count, step_count)
    rim_all = lax.all_to_all(rims, "tm", split_axis=0, concat_axis=0, tiled=True)
    extent = lax.dynamic_slice_in_dim(depth_extent, lax.axis_index("tm"), 1, 0)
    return image(extent, q_rate, src_all, rcv_all, rim_all)


def solution(mesh):
    placed = (P("tile", "tm", None, None), P("tile", "tm", None, None), P(), P(), P(), P("tile"))
    return jax.shard_map(
        local,
        mesh=mesh,
        in_specs=placed,
        out_specs=P(("tile", "tm"), None, None, None),
        check_vma=False,
    )
```

```python
import functools
import math

import jax
import jax.numpy as jnp
from jax import lax
from jax.experimental import pallas as pl
from jax.experimental.pallas import tpu as pltpu
from jax.sharding import PartitionSpec as P

GSTEP = 16
GB = 8
OFFS = 49
RIM = 16
BODY = OFFS - 1


def pack_kernel(send_ref, dest_ref, src_lo, src_hi, rcv_lo, rcv_hi, *out_refs, slots, steps):
    tail = out_refs[0].shape[0] - slots * 2 * steps * RIM
    depth = out_refs[0].shape[1]
    row_ids = lax.broadcasted_iota(jnp.int32, (tail, depth), 0)
    for shift, out_ref in enumerate(out_refs):
        dest = dest_ref[shift]
        extra = jnp.zeros((tail, depth), jnp.float32)
        for slot in range(slots):
            choice = send_ref[dest * slots + slot]
            index = choice // 2
            right = choice % 2
            for field, (low, high) in enumerate(((src_lo, src_hi), (rcv_lo, rcv_hi))):
                for step in range(steps):
                    at = (slot * 2 + field) * steps + step
                    rows = low[index, step]
                    rim = jnp.where(right == 1, rows[:RIM], high[index, step])
                    out_ref[at * RIM : (at + 1) * RIM, :] = rim
                    beyond = rows[RIM : RIM + 8].astype(jnp.float32)[0:1]
                    extra = jnp.where(row_ids == at, beyond, extra)
        out_ref[slots * 2 * steps * RIM :, :] = extra.astype(out_ref.dtype)


def pack(send, dest, src_snap, rcv_snap, slots):
    tiles, steps, width, depth = src_snap.shape
    devices = dest.shape[0]
    parts = slots * 2 * steps
    rows = parts * RIM + -(-parts // 16) * 16
    low = pl.BlockSpec((tiles, steps, RIM + 8, depth), lambda i, s, d: (0, 0, 0, 0))
    high = pl.BlockSpec((tiles, steps, RIM, depth), lambda i, s, d: (0, 0, width // RIM - 1, 0))
    return pl.pallas_call(
        functools.partial(pack_kernel, slots=slots, steps=steps),
        name="pack_rims",
        grid_spec=pltpu.PrefetchScalarGridSpec(
            num_scalar_prefetch=2,
            grid=(1,),
            in_specs=[low, high, low, high],
            out_specs=[pl.BlockSpec((rows, depth), lambda i, s, d: (0, 0))] * devices,
        ),
        out_shape=[jax.ShapeDtypeStruct((rows, depth), src_snap.dtype)] * devices,
    )(send, dest, src_snap, src_snap, rcv_snap, rcv_snap)


def unpack_kernel(arrival_ref, *refs, devices, slots, steps):
    in_refs, out_ref, all_ref = refs[:devices], refs[-2], refs[-1]
    for device, in_ref in enumerate(in_refs):
        all_ref[device] = in_ref[...]
    rows = 2 * steps * RIM
    count = 2 * steps
    for tile in range(out_ref.shape[0]):
        left = arrival_ref[2 * tile]
        right = arrival_ref[2 * tile + 1]
        left_device, left_slot = left // slots, left % slots
        right_device, right_slot = right // slots, right % slots
        out_ref[tile, 0:rows, :] = all_ref[left_device, pl.ds(pl.multiple_of(left_slot * rows, 16), rows), :]
        out_ref[tile, rows : 2 * rows, :] = all_ref[
            right_device, pl.ds(pl.multiple_of(right_slot * rows, 16), rows), :
        ]
        tail = all_ref[right_device, slots * rows :, :].astype(jnp.float32)
        picked = tail[0:count]
        for slot in range(1, slots):
            picked = jnp.where(right_slot == slot, tail[slot * count : (slot + 1) * count], picked)
        first = [
            out_ref[tile, rows + at * RIM : rows + at * RIM + 8, :].astype(jnp.float32)[0:1]
            for at in range(count)
        ]
        out_ref[tile, 2 * rows :, :] = jnp.concatenate([picked, *first], axis=0).astype(out_ref.dtype)


def unpack(arrival, received, slots, tiles, steps):
    devices = len(received)
    in_rows, depth = received[0].shape
    dtype = received[0].dtype
    rows = 2 * (2 * steps * RIM) + 4 * steps
    return pl.pallas_call(
        functools.partial(unpack_kernel, devices=devices, slots=slots, steps=steps),
        name="unpack_rims",
        grid_spec=pltpu.PrefetchScalarGridSpec(
            num_scalar_prefetch=1,
            grid=(1,),
            in_specs=[pl.BlockSpec((in_rows, depth), lambda i, s: (0, 0))] * devices,
            out_specs=pl.BlockSpec((tiles, rows, depth), lambda i, s: (0, 0, 0)),
            scratch_shapes=[pltpu.VMEM((devices, in_rows, depth), dtype)],
        ),
        out_shape=jax.ShapeDtypeStruct((tiles, rows, depth), dtype),
    )(arrival, *received)


def inner_kernel(
    q_ref, main_ref, out_ref, side_ref, rev_ref, fwd_ref, body_ref, last_ref, *, total_steps, parts
):
    devices, fields, width, _ = main_ref.shape
    steps = fields // 2
    strip = width + 2 * RIM
    rows = 2 * steps * RIM
    many = parts * steps
    body_ref[...] = jnp.zeros_like(body_ref)
    last_ref[...] = jnp.zeros_like(last_ref)
    fwd_ref[...] = jnp.zeros_like(fwd_ref)

    out_rows = rev_ref.shape[1]
    out_id = lax.broadcasted_iota(jnp.int32, (out_rows, width), 0)
    in_id = lax.broadcasted_iota(jnp.int32, (out_rows, width), 1) + RIM
    flip = (out_id <= strip) & (in_id == strip - out_id)
    pick = (out_id >= strip + 8) & (in_id == (out_id - (strip + 8)) * GSTEP)
    select = (flip | pick).astype(main_ref.dtype)
    pick_rows = 2 * RIM + 2 * 8
    row = lax.broadcasted_iota(jnp.int32, (pick_rows, width), 0)
    cell = lax.broadcasted_iota(jnp.int32, (pick_rows, width), 1)
    meet = jnp.where(row < RIM, 2 * RIM - row, width - row)
    meet = jnp.where(row == 2 * RIM, width - 2 * RIM, meet)
    meet = jnp.where(row == 2 * RIM + 1, width - 3 * RIM, meet)
    ends = (row - (2 * RIM + 8)) * GSTEP + BODY - RIM
    meet = jnp.where(row >= 2 * RIM + 8, ends, meet)
    side_pick = (cell == meet).astype(main_ref.dtype)

    def block(number, carry):
        for part in range(parts):
            source = number * parts + part
            for step in range(steps):
                at = part * steps + step
                time = (source * steps + step).astype(jnp.float32)
                weight = jnp.exp(q_ref[...] * time / total_steps)
                own_src = main_ref[source, step]
                own_rcv = main_ref[source, steps + step]
                rev_ref[at] = jnp.dot(select, own_src, preferred_element_type=jnp.float32)
                fwd_ref[at, RIM : RIM + width, :] = own_rcv.astype(jnp.float32) * weight
                for group, own in enumerate((own_rcv, own_src)):
                    chosen = jnp.dot(side_pick, own, preferred_element_type=jnp.float32) * weight
                    low = (group * steps + step) * RIM
                    one = group * steps + step
                    side_ref[source, low : low + RIM, :] = chosen[0:RIM]
                    side_ref[source, rows + low : rows + low + RIM, :] = chosen[RIM : 2 * RIM]
                    side_ref[source, 2 * rows + one : 2 * rows + one + 1, :] = chosen[2 * RIM : 2 * RIM + 1]
                    one += 2 * rows + 2 * steps
                    side_ref[source, one : one + 1, :] = chosen[2 * RIM + 1 : 2 * RIM + 2]
                    if group == 0:
                        fwd_ref[at, strip + 8 : strip + 16, :] = chosen[2 * RIM + 8 :]
        for gather in range(GB):
            rev_at = strip - BODY - GSTEP * gather
            fwd_at = GSTEP * gather
            total = body_ref[gather]
            for at in range(many):
                total += rev_ref[at, rev_at : rev_at + BODY, :] * fwd_ref[at, fwd_at : fwd_at + BODY, :]
            body_ref[gather] = total
        total = last_ref[...]
        for at in range(many):
            total += rev_ref[at, strip + 8 : strip + 16, :] * fwd_ref[at, strip + 8 : strip + 16, :]
        last_ref[...] = total
        return carry

    lax.fori_loop(0, devices // parts, block, 0)
    for gather in range(GB):
        out_ref[0:BODY, gather, :] = body_ref[gather]
    out_ref[BODY, :, :] = last_ref[...]


def inner(q_rate, both):
    devices, fields, width, depth = both.shape
    steps = fields // 2
    parts = 2
    strip = width + 2 * RIM
    side_rows = 4 * steps * RIM + 4 * steps
    return pl.pallas_call(
        functools.partial(inner_kernel, total_steps=devices * steps, parts=parts),
        name="inner_cells",
        grid=(1,),
        in_specs=[
            pl.BlockSpec((1, depth), lambda i: (0, 0)),
            pl.BlockSpec(both.shape, lambda i: (0, 0, 0, 0)),
        ],
        out_specs=[
            pl.BlockSpec((OFFS, GB, depth), lambda i: (0, 0, 0)),
            pl.BlockSpec((devices, side_rows, depth), lambda i: (0, 0, 0)),
        ],
        scratch_shapes=[
            pltpu.VMEM((parts * steps, strip + 16, depth), jnp.float32),
            pltpu.VMEM((parts * steps, strip + 16, depth), jnp.float32),
            pltpu.VMEM((GB, BODY, depth), jnp.float32),
            pltpu.VMEM((GB, depth), jnp.float32),
        ],
        out_shape=[
            jax.ShapeDtypeStruct((OFFS, GB, depth), jnp.float32),
            jax.ShapeDtypeStruct((devices, side_rows, depth), jnp.float32),
        ],
    )(q_rate.reshape(1, depth), both)


def outer_kernel(extent_ref, in_ref, side_ref, rim_ref, out_ref, *, steps, norm):
    devices, side_rows, depth = side_ref.shape
    rows = 2 * steps * RIM
    depth_id = lax.broadcasted_iota(jnp.int32, (1, depth), 1)
    scale = jnp.where(depth_id < extent_ref[0], norm, 0.0)
    out_ref[...] = in_ref[...] * scale

    def total(low, high):
        kept = jnp.zeros((high - low, depth), jnp.float32)
        for device in range(devices):
            kept += side_ref[device, low:high, :] * rim_ref[device, low:high, :].astype(jnp.float32)
        return kept * scale

    def put(offset, gather, value):
        out_ref[offset, gather : gather + 1, :] += value

    width_steps = steps * RIM
    for base, gather, falls, rises in ((0, 0, BODY, 0), (rows, GB - 1, RIM, 2 * RIM)):
        for field in range(2):
            found = total(base + field * width_steps, base + (field + 1) * width_steps)
            found = sum(found[step * RIM : (step + 1) * RIM] for step in range(steps))
            for cell in range(RIM):
                put(falls - cell if field == 0 else rises + cell, gather, found[cell : cell + 1])
    found = total(2 * rows, side_rows)
    for one, (offset, gather) in enumerate(((0, GB - 1), (BODY, GB - 1), (0, GB - 2), (BODY, GB - 2))):
        low = one * steps
        put(offset, gather, sum(found[low + step : low + step + 1] for step in range(steps)))


def outer(extent, part, side, rims):
    devices, side_rows, _ = side.shape
    steps = side_rows // (4 * RIM + 4)
    by_offset = pl.pallas_call(
        functools.partial(outer_kernel, steps=steps, norm=1.0 / math.sqrt(devices * steps)),
        name="rim_cells",
        grid_spec=pltpu.PrefetchScalarGridSpec(
            num_scalar_prefetch=1,
            grid=(1,),
            in_specs=[
                pl.BlockSpec(part.shape, lambda i, s: (0, 0, 0)),
                pl.BlockSpec(side.shape, lambda i, s: (0, 0, 0)),
                pl.BlockSpec(rims.shape, lambda i, s: (0, 0, 0)),
            ],
            out_specs=pl.BlockSpec(part.shape, lambda i, s: (0, 0, 0)),
        ),
        out_shape=jax.ShapeDtypeStruct(part.shape, part.dtype),
    )(extent, part, side, rims)
    return by_offset.transpose(1, 0, 2)[None]


def routes(nbr_device, nbr_index, device_count, tile_count, slots, own_index):
    requests = 2 * tile_count
    device = nbr_device.reshape(device_count, requests)
    code = nbr_index.reshape(device_count, requests) * 2 + jnp.arange(requests, dtype=jnp.int32) % 2
    ids = jnp.arange(requests, dtype=jnp.int32)
    named = device == own_index
    rank = jnp.sum((named[:, None, :] & (ids[None, :] < ids[:, None])).astype(jnp.int32), axis=2)
    hit = named[:, None, :] & (rank[:, None, :] == jnp.arange(slots, dtype=jnp.int32)[None, :, None])
    send = jnp.sum(jnp.where(hit, code[:, None, :], 0), axis=2).reshape(-1)
    mine = lax.dynamic_slice_in_dim(device, own_index, 1, 0)[0]
    same = (mine[:, None] == mine[None, :]) & (ids[None, :] < ids[:, None])
    rank_here = jnp.sum(same.astype(jnp.int32), axis=1)
    return send, mine, rank_here


def local(src_snap, rcv_snap, q_rate, nbr_device, nbr_index, depth_extent):
    tile_count, step_count, _, _ = src_snap.shape
    device_count = lax.axis_size("tile")
    slots = (2 * tile_count + device_count - 1) // device_count + 1
    own = lax.axis_index("tile")
    send, mine, rank_here = routes(nbr_device, nbr_index, device_count, tile_count, slots, own)

    count = device_count // 2
    moves = [(major, minor) for major in range(count) for minor in range(2)]
    ids = jnp.arange(device_count, dtype=jnp.int32)
    dest = (own // 2 + ids // 2) % count * 2 + (own % 2 + ids % 2) % 2
    arrival = ((own // 2 - mine // 2) % count * 2 + (own % 2 - mine % 2) % 2) * slots + rank_here

    both = jnp.concatenate([src_snap, rcv_snap], axis=1)
    both = lax.all_to_all(both, "tm", split_axis=0, concat_axis=0, tiled=True)
    packed = pack(send, dest, src_snap, rcv_snap, slots)
    received = [packed[0]]
    for piece, (major, minor) in zip(packed[1:], moves[1:]):
        pairs = [
            (high * 2 + low, (high + major) % count * 2 + (low + minor) % 2)
            for high in range(count)
            for low in range(2)
        ]
        received.append(lax.ppermute(piece, "tile", pairs))
    rims = unpack(arrival, received, slots, tile_count, step_count)
    rim_all = lax.all_to_all(rims, "tm", split_axis=0, concat_axis=0, tiled=True)
    part, side = inner(q_rate, both)
    extent = lax.dynamic_slice_in_dim(depth_extent, lax.axis_index("tm"), 1, 0)
    return outer(extent, part, side, rim_all)


def solution(mesh):
    placed = (P("tile", "tm", None, None), P("tile", "tm", None, None), P(), P(), P(), P("tile"))
    return jax.shard_map(
        local,
        mesh=mesh,
        in_specs=placed,
        out_specs=P(("tile", "tm"), None, None, None),
        check_vma=False,
    )
```
